768 devices in a mesh: blk: 192 (over z_hi, x, y, core), fsdp: 4 (over z_lo).
Axes of the slice: x: 4, y: 8, z: 12 (z_hi: 3, z_lo: 4; z = z_hi * 4 + z_lo), core: 2. Of those that a mesh axis runs over, the one named last changes fastest.
Arguments:
- hidden_in: bfloat16 [4, 98304, 2048], P('fsdp', 'blk'), may hold values from -6 to 6
- w_query: bfloat16 [2048, 128], P('fsdp'), may hold values from -0.125 to 0.125
- query_gain: float32 [128], replicated, may hold values from 0.1 to 1.9
- key_rows: bfloat16 [4, 98304, 128], P('fsdp', 'blk'), may hold values from -4 to 4
- value_rows: bfloat16 [4, 98304, 128], P('fsdp', 'blk'), may hold values from -6 to 6
- grad_out: bfloat16 [4, 98304, 128], P('fsdp', 'blk'), may hold values from -6 to 6
- logsumexp: float32 [4, 98304], P('fsdp', 'blk'), may hold values from 4 to 8
- row_delta: float32 [4, 98304], P('fsdp', 'blk'), may hold values from -6 to 6
- doc_ids: int32 [4, 98304], P('fsdp', 'blk'), may hold values from 0 to 95, never falling along the last dimension, each value on 1 to 4096 neighbouring positions
Outputs:
- grad_hidden: bfloat16 [4, 98304, 2048], P('fsdp', 'blk')
- grad_keys: bfloat16 [4, 98304, 128], P('fsdp', 'blk')
- grad_values: bfloat16 [4, 98304, 128], P('fsdp', 'blk')
- grad_wquery: float32 [2048, 128], P('fsdp')
The draws below stay inside these ranges and needn't reach their ends.
Inputs may be any that keep to these rules, and one draw needn't show every extreme that they name: `doc_ids`: along each sequence the document numbers never fall; each document has 1 to 4096 tokens.
All inputs are finite; a program needn't handle non-finite values.
Results may differ from the reference program's by a relative error of at most 0.0097.
Values may be sent and summed in bfloat16 or wider, within the bound.
A program may use at most 64 MiB of HBM per device.

```python
import math
import jax
import jax.numpy as jnp
import numpy as np
from jax import lax

D = 2048
HD = 128
TOK_DEV = 512
ROUNDS = 8
SEQS = 4
LEN = 98304
DOCS = 96
DOC_MOST = 4096
N_BLK = 192


def steps_of(rng, extent, pieces, low, largest):
    def one(dim, blocks):
        draws = jax.random.uniform(jax.random.fold_in(jax.random.fold_in(rng, 6), dim), (blocks,), jnp.float32, low / len(pieces), largest / len(pieces))
        return jnp.repeat(jnp.exp(draws), extent[dim] // blocks).reshape((-1,) + (1,) * (len(extent) - dim - 1))

    factor_of = one(*pieces[0])
    for cut in pieces[1:]:
        factor_of = factor_of * one(*cut)
    return factor_of


def split_up(amount, total, bound, slope):
    loads = [(1 << 20) // math.isqrt(rank ** slope) + 1 for rank in range(2, amount + 1)]
    rest, holding = total - bound - (amount - 1), [1] * (amount - 1)
    while rest > 0:
        free = [i for i in range(amount - 1) if holding[i] < bound]
        mass, left = sum([loads[i] for i in free]), rest
        for i in free:
            more = min(bound - holding[i], max(1, left * loads[i] // mass), rest)
            holding[i] = holding[i] + more
            rest = rest - more
    return np.array([bound] + holding)


def uneven(own_key, count, total, bound, lean):
    if count == 2:
        one = jax.random.randint(own_key, (), max(1, total - bound), min(bound, total - 1) + 1)
        return jnp.stack([one, total - one])
    lengths = jnp.asarray(split_up(count, total, bound, lean), jnp.int32)
    pairs = (count - 1) // 2
    source_of, receiver = lengths[1:1 + 2 * pairs:2], lengths[2:2 + 2 * pairs:2]
    slack = jnp.minimum(source_of - 1, bound - receiver)
    passed = jax.random.randint(jax.random.fold_in(own_key, 1), (pairs,), 0, 1 << 20) % (slack + 1)
    lengths = lengths.at[1:1 + 2 * pairs:2].set(source_of - passed).at[2:2 + 2 * pairs:2].set(receiver + passed)
    return lengths[jax.random.permutation(jax.random.fold_in(own_key, 2), count)]


def scatter_about(stream_key, dims, spread, bound, shards=(), held_as=jnp.bfloat16):
    gain = steps_of(stream_key, dims, shards, -0.22, 0.18) if shards else 1.0
    drawn = jax.random.normal(stream_key, dims, jnp.float32) * spread * gain
    return jnp.minimum(jnp.maximum(drawn, -bound), bound).astype(held_as)


def setup_inputs(seed: int = 0) -> dict:
    splits = jax.random.split(jax.random.key(seed), 10)
    return {
        "hidden_in": scatter_about(splits[0], (SEQS, LEN, D), 1.0, 6.0, ((0, 4), (1, 192))),
        "w_query": scatter_about(splits[1], (D, HD), D ** -0.5, 0.125, ((0, 4),)),
        "query_gain": jnp.clip(1.0 + 0.18 * jax.random.normal(splits[2], (HD,), jnp.float32), 0.1, 1.9),
        "key_rows": scatter_about(splits[3], (SEQS, LEN, HD), 1.0, 4.0, ((0, 4), (1, 192))),
        "value_rows": scatter_about(splits[4], (SEQS, LEN, HD), 1.0, 6.0, ((0, 4), (1, 192))),
        "grad_out": scatter_about(splits[5], (SEQS, LEN, HD), 1.0, 6.0, ((0, 4), (1, 192))),
        "logsumexp": jnp.clip(4.0 + 4.0 * jax.random.uniform(splits[6], (SEQS, LEN), jnp.float32) ** steps_of(splits[6], (SEQS, LEN), ((0, 4), (1, 192)), -0.2, 0.2), 4.0, 8.0),
        "row_delta": scatter_about(splits[7], (SEQS, LEN), 1.0, 6.0, ((0, 4), (1, 192)), jnp.float32),
        "doc_ids": jax.vmap(lambda own: jnp.searchsorted(jnp.cumsum(uneven(own, DOCS, LEN, DOC_MOST, 2)), jnp.arange(LEN), side="right"))(jax.random.split(splits[8], SEQS)).reshape((SEQS, LEN)).astype(jnp.int32),
    }


def reference(hidden_in, w_query, query_gain, key_rows, value_rows, grad_out, logsumexp, row_delta, doc_ids):
    score_scale = HD ** (-0.5)
    span = ROUNDS * TOK_DEV
    margin = (ROUNDS - 1) * TOK_DEV
    lower_tri = jnp.arange(TOK_DEV, dtype=jnp.int32)[:, None] + margin >= jnp.arange(span, dtype=jnp.int32)[None, :]
    hidden_list = []
    keys_list = []
    values_list = []
    weight_total = jnp.zeros((D, HD), jnp.float32)
    for seq_index in range(SEQS):
        inputs = hidden_in[seq_index]
        q_pre = jnp.dot(inputs, w_query, preferred_element_type=jnp.float32)
        inverse = lax.rsqrt(lax.optimization_barrier(jnp.mean(q_pre * q_pre, axis=-1, keepdims=True)) + 1e-06)
        normed = q_pre * inverse
        query = (normed * query_gain).astype(jnp.bfloat16)
        key_pad = jnp.concatenate([jnp.zeros((margin, HD), key_rows.dtype), key_rows[seq_index]], 0)
        value_pad = jnp.concatenate([jnp.zeros((margin, HD), value_rows.dtype), value_rows[seq_index]], 0)
        doc_pad = jnp.concatenate([-jnp.ones((margin,), jnp.int32), doc_ids[seq_index].astype(jnp.int32)], 0)
        outgrad = grad_out[seq_index]
        lse_row = logsumexp[seq_index]
        delta_row = row_delta[seq_index]
        doc_row = doc_ids[seq_index].astype(jnp.int32)

        def block_step(carry, block):
            keys_acc, values_acc = carry
            start = (block * TOK_DEV).astype(jnp.int32)
            q_block = lax.dynamic_slice_in_dim(query, start, TOK_DEV, 0)
            o_block = lax.dynamic_slice_in_dim(outgrad, start, TOK_DEV, 0)
            l_block = lax.dynamic_slice_in_dim(lse_row, start, TOK_DEV, 0)
            d_block = lax.dynamic_slice_in_dim(delta_row, start, TOK_DEV, 0)
            s_block = lax.dynamic_slice_in_dim(doc_row, start, TOK_DEV, 0)
            k_window = lax.dynamic_slice_in_dim(key_pad, start, span, 0)
            v_window = lax.dynamic_slice_in_dim(value_pad, start, span, 0)
            s_window = lax.dynamic_slice_in_dim(doc_pad, start, span, 0)
            allowed = (s_block[:, None] == s_window[None, :]) & lower_tri
            scores = lax.dot_general(q_block, k_window, (((1,), (1,)), ((), ())), preferred_element_type=jnp.float32) * score_scale
            attn_prob = jnp.exp(jnp.where(allowed, scores - l_block[:, None], -1e+30))
            grad_prob = lax.dot_general(o_block, v_window, (((1,), (1,)), ((), ())), preferred_element_type=jnp.float32)
            grad_score = attn_prob * (grad_prob - d_block[:, None])
            prob_half = attn_prob.astype(jnp.bfloat16)
            score_half = grad_score.astype(jnp.bfloat16)
            query_term = jnp.dot(score_half, k_window, preferred_element_type=jnp.float32)
            key_term = lax.dot_general(score_half, q_block, (((0,), (0,)), ((), ())), preferred_element_type=jnp.float32)
            value_term = lax.dot_general(prob_half, o_block, (((0,), (0,)), ((), ())), preferred_element_type=jnp.float32)
            keys_acc = lax.dynamic_update_slice_in_dim(keys_acc, lax.dynamic_slice_in_dim(keys_acc, start, span, 0) + key_term, start, 0)
            values_acc = lax.dynamic_update_slice_in_dim(values_acc, lax.dynamic_slice_in_dim(values_acc, start, span, 0) + value_term, start, 0)
            return ((keys_acc, values_acc), query_term)
        zeros_pad = jnp.zeros((margin + LEN, HD), jnp.float32)
        (keys_acc, values_acc), query_blocks = lax.scan(block_step, (zeros_pad, zeros_pad), jnp.arange(N_BLK, dtype=jnp.int32))
        grad_query = query_blocks.reshape(LEN, HD) * score_scale
        keys_list.append((keys_acc[margin:] * score_scale).astype(jnp.bfloat16))
        values_list.append(values_acc[margin:].astype(jnp.bfloat16))
        scaled = grad_query * query_gain
        grad_pre = (inverse * (scaled - normed * lax.optimization_barrier(jnp.mean(scaled * normed, axis=-1, keepdims=True)))).astype(jnp.bfloat16)
        hidden_list.append(lax.dot_general(grad_pre, w_query, (((1,), (1,)), ((), ())), preferred_element_type=jnp.float32).astype(jnp.bfloat16))
        weight_total = weight_total + lax.dot_general(inputs, grad_pre, (((0,), (0,)), ((), ())), preferred_element_type=jnp.float32)
    return (jnp.stack(hidden_list), jnp.stack(keys_list), jnp.stack(values_list), weight_total)
```

```python
import jax
import jax.numpy as jnp
from jax import lax
from jax.experimental import pallas as pl
from jax.experimental.pallas import tpu as pltpu
from jax.sharding import PartitionSpec as P

ROUNDS = 8
LAG = 3
NX, NY, NZ, NF = 4, 8, 12, 4
PLANE = NX * NY * 2
MESH = pl.DeviceIdType.MESH
BF = jnp.bfloat16
F32 = jnp.float32
NT = (((1,), (1,)), ((), ()))
TILE = 128


def copy_to(src, dst, send, recv, blk, fsdp):
    return pltpu.make_async_remote_copy(
        src_ref=src, dst_ref=dst, send_sem=send, recv_sem=recv,
        device_id={"blk": blk, "fsdp": fsdp}, device_id_type=MESH)


def wide(column):
    return jnp.concatenate([column] * 4, axis=1)


def main_kernel(
    h_hbm, w_ref, gain_ref, k_ref, v_ref, do_ref, lse_ref, delta_ref, docs_ref,
    gp_ref, wfull, dk_ref, dv_ref, g3,
    h_ref, kb, vb, cb, ob, lb, eb, sb, qb,
    q_own, inv_s, normed_s, lse_c, delta_c, docs_c, dq_acc, dk_acc, dv_acc,
    own_half, csend, crecv, acc_s, xs, xr, a2_s, ys, yr, zs, zr, g1, g2,
    h_sem, f_send, f_recv, b_send, b_recv, fh_send, bh_send, q_send, q_recv, qh_send,
    w_send, w_recv, wc_send, wc_recv, c_sem, x_send, x_recv, y_send, y_recv, z_send, z_recv,
    gy_send, gy_recv, gx_send, gx_recv, gc_sem,
):
    p = lax.axis_index("blk")
    f = lax.axis_index("fsdp")
    last = lax.axis_size("blk") - 1
    c = lax.rem(p, 2)
    y = lax.rem(p // 2, NY)
    x = lax.rem(p // (2 * NY), NX)
    zh = p // PLANE
    z = zh * NF + f
    inpl = lax.rem(p, PLANE)
    scale = 128 ** -0.5

    def at_y(k):
        return p - 2 * y + 2 * lax.rem(y + k, NY)

    def at_x(k):
        return p - 2 * NY * x + 2 * NY * lax.rem(x + k, NX)

    def at_z(k):
        zz = lax.rem(z + k, NZ)
        return inpl + PLANE * (zz // NF), lax.rem(zz, NF)

    partner = p + 1 - 2 * c
    load_h = pltpu.make_async_copy(h_hbm, h_ref, h_sem)
    load_h.start()

    has_next = jnp.logical_and(p < last, inpl != PLANE - 1)
    has_prev = inpl != 0
    fwd_home = jnp.logical_and(inpl >= PLANE - 7, p + 7 <= last)
    bwd_home = jnp.logical_and(inpl < 7, p >= 7)
    fwd_gate = jnp.logical_and(inpl == 0, p > 0)
    bwd_gate = jnp.logical_and(inpl == PLANE - 1, p < last)
    fwd_to = (zh + 1) * PLANE
    bwd_to = zh * PLANE - 1

    barrier = pltpu.get_barrier_semaphore()

    def greet(blk, fsdp):
        pl.semaphore_signal(
            barrier, inc=1, device_id={"blk": blk, "fsdp": fsdp}, device_id_type=MESH)

    greet(partner, f)
    for k in range(1, NY):
        greet(at_y(k), f)
    for k in range(1, NX):
        greet(at_x(k), f)
    for k in range(1, NZ):
        greet(*at_z(k))
    pl.when(has_next)(lambda: greet(p + 1, f))
    pl.when(has_prev)(lambda: greet(p - 1, f))
    pl.when(fwd_home)(lambda: greet(fwd_to, f))
    pl.when(bwd_home)(lambda: greet(bwd_to, f))

    @pl.when(fwd_gate)
    def _():
        for k in range(1, 8):
            greet(p - k, f)

    @pl.when(bwd_gate)
    def _():
        for k in range(1, 8):
            greet(p + k, f)

    def count(flag, n):
        return jnp.where(flag, n, 0)

    pl.semaphore_wait(
        barrier,
        1 + (NY - 1) + (NX - 1) + (NZ - 1) + count(has_next, 1) + count(has_prev, 1)
        + count(fwd_home, 1) + count(bwd_home, 1) + count(fwd_gate, 7) + count(bwd_gate, 7))

    fwd_far = PLANE - inpl
    bwd_far = inpl + 1

    def fwd_step(d, srcs, to, slot, send):
        return [
            copy_to(src, buf.at[slot], send(i), f_recv.at[i, slot], to, f)
            for i, (src, buf) in enumerate(zip(srcs, (kb, vb, cb)))
        ]

    def bwd_step(d, srcs, to, slot, send):
        return [
            copy_to(src, buf.at[slot], send(i), b_recv.at[i, slot], to, f)
            for i, (src, buf) in enumerate(zip(srcs, (ob, lb, eb, sb)))
        ]

    own_fwd = (k_ref, v_ref, docs_ref)
    own_bwd = (do_ref, lse_ref, delta_ref, docs_ref)
    first_fwd = fwd_step(0, own_fwd, p + 1, 1, lambda i: f_send.at[i, 0])
    home_fwd = fwd_step(0, own_fwd, fwd_to, fwd_far, lambda i: fh_send.at[i])
    first_bwd = bwd_step(0, own_bwd, p - 1, 1, lambda i: b_send.at[i, 0])
    home_bwd = bwd_step(0, own_bwd, bwd_to, bwd_far, lambda i: bh_send.at[i])

    def start_all(copies):
        for one in copies:
            one.start()

    def finish_sends(copies):
        for one in copies:
            one.wait_send()

    pl.when(has_next)(lambda: start_all(first_fwd))
    pl.when(fwd_home)(lambda: start_all(home_fwd))
    pl.when(has_prev)(lambda: start_all(first_bwd))
    pl.when(bwd_home)(lambda: start_all(home_bwd))

    half = 256
    mine = pl.ds(pl.multiple_of(c * half, half), half)
    quarter = [pl.ds(pl.multiple_of(c * half + q * 128, 128), 128) for q in range(2)]
    w_copies = []
    for i, (k, rows) in enumerate(
        ((1, mine), (NZ - 1, mine), (2, quarter[0]), (NZ - 2, quarter[1]))
    ):
        w_copies.append(
            copy_to(w_ref.at[rows], wfull.at[f, rows], w_send.at[i], w_recv.at[i], *at_z(k)))
    start_all(w_copies)

    def as_columns(row):
        return jnp.broadcast_to(row, (128, row.shape[1])).T

    lse_c[...] = as_columns(lse_ref[...])
    delta_c[...] = as_columns(delta_ref[...])
    docs_c[...] = as_columns(docs_ref[...].astype(F32)).astype(jnp.int32)
    dk_acc[...] = jnp.zeros_like(dk_acc)
    dv_acc[...] = jnp.zeros_like(dv_acc)

    f1, f2, f3 = lax.rem(f + 1, NF), lax.rem(f + 2, NF), lax.rem(f + 3, NF)
    load_h.wait()
    wfull[f] = w_ref[...]

    def part(fs, w):
        cols = pl.ds(pl.multiple_of(fs * 512, 512), 512)
        return jnp.dot(h_ref[:, cols], w, preferred_element_type=F32)

    q_pre = part(f, w_ref[...])
    wc = [
        copy_to(wfull.at[fs, mine], wfull.at[fs, mine], wc_send.at[i], wc_recv.at[i], partner, f)
        for i, fs in enumerate((f3, f1, f2))
    ]
    w_copies[0].wait_recv()
    wc[0].start()
    w_copies[1].wait_recv()
    wc[1].start()
    w_copies[2].wait_recv()
    w_copies[3].wait_recv()
    wc[2].start()
    for i, fs in enumerate((f3, f1, f2)):
        wc[i].wait_recv()
        q_pre = q_pre + part(fs, wfull[fs])
    inv = lax.rsqrt(jnp.mean(q_pre * q_pre, axis=-1, keepdims=True) + 1e-06)
    normed = q_pre * inv
    q_own[...] = (normed * gain_ref[...]).astype(BF)
    normed_s[...] = normed
    inv_s[...] = jnp.broadcast_to(inv, inv_s.shape)

    def q_step(src, to, slot, send):
        return copy_to(src, qb.at[slot], send, q_recv.at[slot], to, f)

    first_q = q_step(q_own, p - 1, 1, q_send.at[0])
    home_q = q_step(q_own, bwd_to, bwd_far, qh_send)

    def dq_block(keys, values, docs_row, diagonal):
        for t in range(512 // TILE):
            rows = pl.ds(t * TILE, TILE)
            s = lax.dot_general(q_own[rows], keys[...], NT, preferred_element_type=F32) * scale
            allowed = wide(docs_c[rows]) == docs_row[...]
            if diagonal:
                i = lax.broadcasted_iota(jnp.int32, s.shape, 0) + t * TILE
                allowed = allowed & (i >= lax.broadcasted_iota(jnp.int32, s.shape, 1))
            prob = jnp.exp(jnp.where(allowed, s - wide(lse_c[rows]), -1e30))
            dp = lax.dot_general(do_ref[rows], values[...], NT, preferred_element_type=F32)
            ds = (prob * (dp - wide(delta_c[rows]))).astype(BF)
            term = jnp.dot(ds, keys[...], preferred_element_type=F32)
            if diagonal:
                dq_acc[rows] = term
            else:
                dq_acc[rows] += term

    dq_block(k_ref, v_ref, docs_ref, True)
    pl.when(has_prev)(lambda: first_q.start())
    pl.when(bwd_home)(lambda: home_q.start())

    def bwd_arrived(d):
        copies = bwd_step(d, (ob.at[d], lb.at[d], eb.at[d], sb.at[d]), p - 1, d + 1,
                          lambda i: b_send.at[i, d])
        return copies

    def take_q(d):
        @pl.when(p + d <= last)
        def _():
            q_step(q_own, p, d, q_send.at[0]).wait_recv()

        @pl.when(jnp.logical_and(jnp.logical_and(p + d <= last, has_prev), d < 7))
        def _():
            nxt = jnp.minimum(d + 1, 7)
            q_step(qb.at[d], p - 1, nxt, q_send.at[d]).start()

    def chain(d, carry):
        nxt = jnp.minimum(d + 1, 7)
        have_f = p >= d
        have_b = p + d <= last
        pass_f = jnp.logical_and(jnp.logical_and(have_f, has_next), d < 7)
        pass_b = jnp.logical_and(jnp.logical_and(have_b, has_prev), d < 7)
        fwd = fwd_step(d, (kb.at[d], vb.at[d], cb.at[d]), p + 1, nxt, lambda i: f_send.at[i, d])
        bwd = bwd_step(d, (ob.at[d], lb.at[d], eb.at[d], sb.at[d]), p - 1, nxt,
                       lambda i: b_send.at[i, d])
        f_in = fwd_step(d, own_fwd, p, d, lambda i: f_send.at[i, 0])
        b_in = bwd_step(d, own_bwd, p, d, lambda i: b_send.at[i, 0])
        for i in range(3):
            pl.when(have_f)(lambda: f_in[i].wait_recv())
            pl.when(pass_f)(lambda: fwd[i].start())
        for i in range(4):
            pl.when(have_b)(lambda: b_in[i].wait_recv())
            pl.when(pass_b)(lambda: bwd[i].start())
        pl.when(d > LAG)(lambda: take_q(d - LAG))
        pl.when(have_f)(lambda: dq_block(kb.at[d], vb.at[d], cb.at[d], False))
        return carry

    lax.fori_loop(1, 8, chain, 0)

    g = dq_acc[...] * scale * gain_ref[...]
    nrm = normed_s[...]
    grad_pre = inv_s[...] * (g - nrm * jnp.mean(g * nrm, axis=-1, keepdims=True))
    gp_ref[...] = grad_pre.astype(BF)
    gp_t = grad_pre.T.astype(BF)

    def product(side, fs):
        cols = pl.ds(pl.multiple_of(fs * 512 + side * 256, 256), 256)
        return jnp.dot(gp_t, h_ref[:, cols], preferred_element_type=F32)

    def dkv_block(q_ref, o_ref, lse_row, delta_row, docs_row, diagonal):
        for t in range(512 // TILE):
            rows = pl.ds(t * TILE, TILE)
            s = lax.dot_general(k_ref[rows], q_ref[...], NT, preferred_element_type=F32) * scale
            allowed = wide(docs_c[rows]) == docs_row[...]
            if diagonal:
                i = lax.broadcasted_iota(jnp.int32, s.shape, 0) + t * TILE
                allowed = allowed & (i <= lax.broadcasted_iota(jnp.int32, s.shape, 1))
            prob = jnp.exp(jnp.where(allowed, s - lse_row[...], -1e30))
            dp = lax.dot_general(v_ref[rows], o_ref[...], NT, preferred_element_type=F32)
            ds = (prob * (dp - delta_row[...])).astype(BF)
            dv_acc[rows] += jnp.dot(prob.astype(BF), o_ref[...], preferred_element_type=F32)
            dk_acc[rows] += jnp.dot(ds, q_ref[...], preferred_element_type=F32)

    def filler(lo, hi):
        def one(d, carry):
            pl.when(p + d <= last)(
                lambda: dkv_block(qb.at[d], ob.at[d], lb.at[d], eb.at[d], sb.at[d], False))
            return carry

        lax.fori_loop(lo, hi, one, 0)

    for fs in range(NF):
        csend[:, fs * 256:(fs + 1) * 256] = product(1 - c, fs).astype(BF)
    to_core = copy_to(csend, crecv, c_sem.at[0], c_sem.at[1], partner, f)
    to_core.start()
    take_q(5)
    for fs in range(NF):
        own_half[:, fs * 256:(fs + 1) * 256] = product(c, fs)
    dkv_block(q_own, do_ref, lse_ref, delta_ref, docs_ref, True)
    to_core.wait_recv()
    acc = own_half[...] + crecv[...].astype(F32)
    acc_s[...] = acc
    for xx in range(NX):
        xs[xx] = acc[32 * xx:32 * xx + 32].astype(BF)
    x_copies = [
        copy_to(xs.at[lax.rem(x + k, NX)], xr.at[k - 1], x_send.at[k - 1], x_recv.at[k - 1],
                at_x(k), f)
        for k in range(1, NX)
    ]
    start_all(x_copies)
    take_q(6)
    filler(1, 3)
    a2 = acc_s[pl.ds(pl.multiple_of(32 * x, 32), 32), :]
    for k in range(NX - 1):
        x_copies[k].wait_recv()
        a2 = a2 + xr[k].astype(F32)
    for yy in range(NY):
        for fs in range(NF):
            col = fs * 256 + 128 * (yy % 2)
            ys[yy, 8 * fs:8 * fs + 8] = a2[8 * (yy // 2):8 * (yy // 2) + 8, col:col + 128]
    y_copies = [
        copy_to(ys.at[lax.rem(y + k, NY)], yr.at[k - 1], y_send.at[k - 1], y_recv.at[k - 1],
                at_y(k), f)
        for k in range(1, NY)
    ]
    start_all(y_copies)
    take_q(7)
    filler(3, 5)
    a3 = ys[y]
    for k in range(NY - 1):
        y_copies[k].wait_recv()
        a3 = a3 + yr[k]
    zs[...] = a3
    z_copies = []
    for k in range(1, NZ):
        blk, fz = at_z(k)
        z_copies.append(
            copy_to(zs.at[pl.ds(pl.multiple_of(8 * fz, 8), 8)], zr.at[k - 1], z_send.at[k - 1],
                    z_recv.at[k - 1], blk, fz))
    start_all(z_copies)
    filler(5, 8)
    done = zs[pl.ds(pl.multiple_of(8 * f, 8), 8), :]
    for k in range(NZ - 1):
        z_copies[k].wait_recv()
        done = done + zr[k]
    g1[y] = done
    gy = [
        copy_to(g1.at[y], g1.at[y], gy_send.at[k - 1], gy_recv.at[k - 1], at_y(k), f)
        for k in range(1, NY)
    ]
    start_all(gy)
    dk_ref[...] = (dk_acc[...] * scale).astype(BF)
    dv_ref[...] = dv_acc[...].astype(BF)
    for one in gy:
        one.wait_recv()
    gx = [
        copy_to(g1, g2.at[x], gx_send.at[k - 1], gx_recv.at[k - 1], at_x(k), f)
        for k in range(1, NX)
    ]
    start_all(gx)
    g2[x] = g1[...]
    for one in gx:
        one.wait_recv()
    gc = copy_to(g2, g3.at[c], gc_sem.at[0], gc_sem.at[1], partner, f)
    gc.start()
    g3[c] = g2[...]

    pl.when(has_next)(lambda: finish_sends(first_fwd))
    pl.when(fwd_home)(lambda: finish_sends(home_fwd))
    pl.when(has_prev)(lambda: finish_sends(first_bwd))
    pl.when(bwd_home)(lambda: finish_sends(home_bwd))
    pl.when(has_prev)(lambda: first_q.wait_send())
    pl.when(bwd_home)(lambda: home_q.wait_send())
    finish_sends(w_copies)
    finish_sends(wc)

    def drained(d, carry):
        @pl.when(jnp.logical_and(p >= d, has_next))
        def _():
            finish_sends(fwd_step(d, (kb.at[d], vb.at[d], cb.at[d]), p + 1, d + 1,
                                  lambda i: f_send.at[i, d]))

        @pl.when(jnp.logical_and(p + d <= last, has_prev))
        def _():
            finish_sends(bwd_step(d, (ob.at[d], lb.at[d], eb.at[d], sb.at[d]), p - 1, d + 1,
                                  lambda i: b_send.at[i, d]))
            q_step(qb.at[d], p - 1, d + 1, q_send.at[d]).wait_send()

        return carry

    lax.fori_loop(1, 7, drained, 0)
    for group in ([to_core], x_copies, y_copies, z_copies, gy, gx, [gc]):
        finish_sends(group)
    gc.wait_recv()


def final_kernel(gp_ref, w_ref, dk_ref, dv_ref, g_ref, gh_out, dk_out, dv_out, wq_out):
    for fs in range(NF):
        gh_out[:, fs * 512:(fs + 1) * 512] = lax.dot_general(
            gp_ref[...], w_ref[fs], NT, preferred_element_type=F32).astype(BF)
    dk_out[...] = dk_ref[...]
    dv_out[...] = dv_ref[...]
    wq_out[...] = g_ref[...].reshape(128, 128).T


def local(
    hidden_in, w_query, query_gain, key_rows, value_rows, grad_out, logsumexp, row_delta, doc_ids
):
    vmem = pl.BlockSpec(memory_space=pltpu.VMEM)
    sds = jax.ShapeDtypeStruct
    dma = pltpu.SemaphoreType.DMA
    v = pltpu.VMEM
    tok = (512, 128)
    gp, wfull, dk, dv, g3 = pl.pallas_call(
        main_kernel,
        out_shape=[sds(tok, BF), sds((NF, 512, 128), BF), sds(tok, BF), sds(tok, BF),
                   sds((2, NX, NY, 8, 128), F32)],
        in_specs=[pl.BlockSpec(memory_space=pl.ANY)] + [vmem] * 8,
        out_specs=[vmem] * 5,
        scratch_shapes=[
            v((512, 2048), BF), v((8, *tok), BF), v((8, *tok), BF), v((8, 1, 512), jnp.int32),
            v((8, *tok), BF), v((8, 1, 512), F32), v((8, 1, 512), F32),
            v((8, 1, 512), jnp.int32), v((8, *tok), BF),
            v(tok, BF), v(tok, F32), v(tok, F32), v(tok, F32), v(tok, F32),
            v(tok, jnp.int32), v(tok, F32), v(tok, F32), v(tok, F32),
            v((128, 1024), F32), v((128, 1024), BF), v((128, 1024), BF), v((128, 1024), F32),
            v((NX, 32, 1024), BF), v((NX - 1, 32, 1024), BF), v((32, 1024), F32),
            v((NY, 32, 128), F32), v((NY - 1, 32, 128), F32),
            v((32, 128), F32), v((NZ - 1, 8, 128), F32),
            v((NY, 8, 128), F32), v((NX, NY, 8, 128), F32),
            dma, dma((3, 8)), dma((3, 8)), dma((4, 8)), dma((4, 8)), dma((3,)), dma((4,)),
            dma((8,)), dma((8,)), dma,
            dma((4,)), dma((4,)), dma((3,)), dma((3,)), dma((2,)),
            dma((NX - 1,)), dma((NX - 1,)), dma((NY - 1,)), dma((NY - 1,)),
            dma((NZ - 1,)), dma((NZ - 1,)), dma((NY - 1,)), dma((NY - 1,)),
            dma((NX - 1,)), dma((NX - 1,)), dma((2,)),
        ],
        compiler_params=pltpu.CompilerParams(
            collective_id=0, has_side_effects=True, vmem_limit_bytes=48 << 20),
        name="main",
    )(hidden_in[0], w_query, query_gain[None], key_rows[0], value_rows[0], grad_out[0],
      logsumexp, row_delta, doc_ids)

    row = pl.BlockSpec((128, 128), lambda i: (i, 0))
    whole = pl.BlockSpec((NF, 512, 128), lambda i: (0, 0, 0))
    gh, dk, dv, wq = pl.pallas_call(
        final_kernel,
        grid=(4,),
        out_shape=[sds((512, 2048), BF), sds(tok, BF), sds(tok, BF), sds(tok, F32)],
        in_specs=[row, whole, row, row,
                  pl.BlockSpec((1, NX, NY // 2, 1, 8, 128),
                               lambda i: (i // 2, 0, 0, i % 2, 0, 0))],
        out_specs=[pl.BlockSpec((128, 2048), lambda i: (i, 0)), row, row, row],
        name="finish",
    )(gp, wfull, dk, dv, g3.reshape(2, NX, NY // 2, 2, 8, 128))
    return gh[None], dk[None], dv[None], wq


def solution(mesh):
    return jax.shard_map(
        local,
        mesh=mesh,
        in_specs=(
            P("fsdp", "blk", None),
            P("fsdp", None),
            P(),
            P("fsdp", "blk", None),
            P("fsdp", "blk", None),
            P("fsdp", "blk", None),
            P("fsdp", "blk"),
            P("fsdp", "blk"),
            P("fsdp", "blk"),
        ),
        out_specs=(
            P("fsdp", "blk", None),
            P("fsdp", "blk", None),
            P("fsdp", "blk", None),
            P("fsdp", None),
        ),
        check_vma=False,
    )
```

```python
import jax
import jax.numpy as jnp
from jax import lax
from jax.experimental import pallas as pl
from jax.experimental.pallas import tpu as pltpu
from jax.sharding import PartitionSpec as P

ROUNDS = 8
LAG = 3
NX, NY, NZ, NF = 4, 8, 12, 4
PLANE = NX * NY * 2
GIVER = {1: 63, 2: 46, 3: 61, 4: 28, 5: 11, 6: 42, 7: 57}
HOME = {d: PLANE - d for d in GIVER}
DIRECT = [d for d in GIVER if GIVER[d] == HOME[d]]
VIA = [d for d in GIVER if GIVER[d] != HOME[d]]
MESH = pl.DeviceIdType.MESH
BF = jnp.bfloat16
F32 = jnp.float32
NT = (((1,), (1,)), ((), ()))
TILE = 512


def copy_to(src, dst, send, recv, blk, fsdp):
    return pltpu.make_async_remote_copy(
        src_ref=src, dst_ref=dst, send_sem=send, recv_sem=recv,
        device_id={"blk": blk, "fsdp": fsdp}, device_id_type=MESH)


def wide(column):
    return jnp.concatenate([column] * 4, axis=1)


def main_kernel(
    h_hbm, w_hbm, gain_hbm, k_hbm, v_hbm, do_hbm, lse_hbm, delta_hbm, docs_hbm,
    gh_ref, dk_ref, dv_ref, g3,
    h_ref, w_ref, gain_ref, k_ref, v_ref, do_ref, lse_ref, delta_ref, docs_ref,
    wfull, gp_ref, kb, vb, cb, ob, lb, eb, sb, qb,
    q_own, inv_s, normed_s, lse_c, delta_c, docs_c, dq_acc, dk_acc, dv_acc,
    own_half, csend, crecv, acc_s, xs, xr, y_own, ys, yr, zs, zr, g1, g2,
    hk, hv, hc, ho, hl, he, hs, hq,
    l_sem, f_send, f_recv, b_send, b_recv, fh_send, bh_send, q_send, q_recv, qh_send,
    hf_send, hf_recv, hb_send, hb_recv,
    w_send, w_recv, wc_send, wc_recv, c_sem, x_send, x_recv, y_send, y_recv, z_send, z_recv,
    gy_send, gy_recv, gx_send, gx_recv, gc_sem,
):
    p = lax.axis_index("blk")
    f = lax.axis_index("fsdp")
    last = lax.axis_size("blk") - 1
    c = lax.rem(p, 2)
    y = lax.rem(p // 2, NY)
    x = lax.rem(p // (2 * NY), NX)
    zh = p // PLANE
    z = zh * NF + f
    inpl = lax.rem(p, PLANE)
    scale = 128 ** -0.5

    def at_y(k):
        return p - 2 * y + 2 * lax.rem(y + k, NY)

    def at_x(k):
        return p - 2 * NY * x + 2 * NY * lax.rem(x + k, NX)

    def at_z(k):
        zz = lax.rem(z + k, NZ)
        return inpl + PLANE * (zz // NF), lax.rem(zz, NF)

    partner = p + 1 - 2 * c
    loads = [
        pltpu.make_async_copy(src, dst, l_sem.at[i])
        for i, (src, dst) in enumerate((
            (w_hbm, w_ref), (h_hbm, h_ref), (k_hbm, k_ref), (v_hbm, v_ref), (do_hbm, do_ref),
            (lse_hbm, lse_ref), (delta_hbm, delta_ref), (docs_hbm, docs_ref),
            (gain_hbm, gain_ref)))
    ]
    for one in loads:
        one.start()

    has_next = jnp.logical_and(p < last, inpl != PLANE - 1)
    has_prev = inpl != 0
    up, down = zh < NZ // NF - 1, zh > 0
    mirror = PLANE - 1 - inpl

    def among(values, at):
        hit = at == values[0]
        for one in values[1:]:
            hit = jnp.logical_or(hit, at == one)
        return hit

    def lookup(pairs, at):
        out = jnp.int32(0)
        for key, value in pairs:
            out = out + jnp.where(at == key, value, 0)
        return out

    def roles(on, at):
        direct = jnp.logical_and(on, among([HOME[d] for d in DIRECT], at))
        via = jnp.logical_and(on, among([HOME[d] for d in VIA], at))
        middle = jnp.logical_and(on, among([GIVER[d] for d in VIA], at))
        to_middle = lookup([(HOME[d], GIVER[d] - HOME[d]) for d in VIA], at)
        to_home = lookup([(GIVER[d], HOME[d] - GIVER[d]) for d in VIA], at)
        slot = lookup([(GIVER[d], d) for d in VIA], at)
        return direct, via, middle, to_middle, to_home, slot

    fwd_direct, fwd_via, fwd_mid, off, back, fwd_slot = roles(up, inpl)
    fwd_mid_at, fwd_home_at = p + off, p + back
    bwd_direct, bwd_via, bwd_mid, off, back, bwd_slot = roles(down, mirror)
    bwd_mid_at, bwd_home_at = p - off, p - back
    fwd_gate = jnp.logical_and(inpl == 0, p > 0)
    bwd_gate = jnp.logical_and(inpl == PLANE - 1, p < last)
    fwd_to = (zh + 1) * PLANE
    bwd_to = zh * PLANE - 1

    barrier = pltpu.get_barrier_semaphore()

    def greet(blk, fsdp):
        pl.semaphore_signal(
            barrier, inc=1, device_id={"blk": blk, "fsdp": fsdp}, device_id_type=MESH)

    greet(partner, f)
    for k in range(1, NY):
        greet(at_y(k), f)
    for k in range(1, NX):
        greet(at_x(k), f)
    for k in range(1, NZ):
        greet(*at_z(k))
    pl.when(has_next)(lambda: greet(p + 1, f))
    pl.when(has_prev)(lambda: greet(p - 1, f))
    pl.when(jnp.logical_or(fwd_direct, fwd_mid))(lambda: greet(fwd_to, f))
    pl.when(jnp.logical_or(bwd_direct, bwd_mid))(lambda: greet(bwd_to, f))
    pl.when(fwd_via)(lambda: greet(fwd_mid_at, f))
    pl.when(fwd_mid)(lambda: greet(fwd_home_at, f))
    pl.when(bwd_via)(lambda: greet(bwd_mid_at, f))
    pl.when(bwd_mid)(lambda: greet(bwd_home_at, f))

    @pl.when(fwd_gate)
    def _():
        for d in GIVER:
            greet(p - PLANE + GIVER[d], f)

    @pl.when(bwd_gate)
    def _():
        for d in GIVER:
            greet(p + PLANE - GIVER[d], f)

    peers = 1 + (NY - 1) + (NX - 1) + (NZ - 1)
    for flag, n in (
        (has_next, 1), (has_prev, 1), (fwd_direct, 1), (bwd_direct, 1), (fwd_mid, 2),
        (bwd_mid, 2), (fwd_via, 1), (bwd_via, 1), (fwd_gate, 7), (bwd_gate, 7),
    ):
        peers = peers + jnp.where(flag, n, 0)
    pl.semaphore_wait(barrier, peers)

    fwd_far = PLANE - inpl
    bwd_far = inpl + 1

    def fwd_step(d, srcs, to, slot, send):
        return [
            copy_to(src, buf.at[slot], send(i), f_recv.at[i, slot], to, f)
            for i, (src, buf) in enumerate(zip(srcs, (kb, vb, cb)))
        ]

    def bwd_step(d, srcs, to, slot, send):
        return [
            copy_to(src, buf.at[slot], send(i), b_recv.at[i, slot], to, f)
            for i, (src, buf) in enumerate(zip(srcs, (ob, lb, eb, sb)))
        ]

    own_fwd = (k_hbm, v_hbm, docs_hbm)
    own_bwd = (do_hbm, lse_hbm, delta_hbm, docs_hbm)
    first_fwd = fwd_step(0, own_fwd, p + 1, 1, lambda i: f_send.at[i, 0])
    home_fwd = fwd_step(0, own_fwd, fwd_to, fwd_far, lambda i: fh_send.at[i])
    via_fwd = [
        copy_to(src, buf, fh_send.at[i], hf_recv.at[i], fwd_mid_at, f)
        for i, (src, buf) in enumerate(zip(own_fwd, (hk, hv, hc)))
    ]
    mid_fwd = fwd_step(0, (hk, hv, hc), fwd_to, fwd_slot, lambda i: hf_send.at[i])
    first_bwd = bwd_step(0, own_bwd, p - 1, 1, lambda i: b_send.at[i, 0])
    home_bwd = bwd_step(0, own_bwd, bwd_to, bwd_far, lambda i: bh_send.at[i])
    via_bwd = [
        copy_to(src, buf, bh_send.at[i], hb_recv.at[i], bwd_mid_at, f)
        for i, (src, buf) in enumerate(zip(own_bwd, (ho, hl, he, hs)))
    ]
    mid_bwd = bwd_step(0, (ho, hl, he, hs), bwd_to, bwd_slot, lambda i: hb_send.at[i])

    def start_all(copies):
        for one in copies:
            one.start()

    def finish_sends(copies):
        for one in copies:
            one.wait_send()

    def hand_on(arriving, leaving):
        for i in range(len(leaving)):
            arriving[i].wait_recv()
            leaving[i].start()

    pl.when(fwd_direct)(lambda: start_all(home_fwd))
    pl.when(fwd_via)(lambda: start_all(via_fwd))
    pl.when(has_next)(lambda: start_all(first_fwd))
    pl.when(bwd_direct)(lambda: start_all(home_bwd))
    pl.when(bwd_via)(lambda: start_all(via_bwd))
    pl.when(has_prev)(lambda: start_all(first_bwd))

    def take_fwd(d):
        nxt = jnp.minimum(d + 1, 7)
        have = p >= d
        onward = jnp.logical_and(jnp.logical_and(have, has_next), d < 7)
        leave = fwd_step(d, (kb.at[d], vb.at[d], cb.at[d]), p + 1, nxt, lambda i: f_send.at[i, d])
        arrive = fwd_step(d, own_fwd, p, d, lambda i: f_send.at[i, 0])
        for i in range(3):
            pl.when(have)(lambda: arrive[i].wait_recv())
            pl.when(onward)(lambda: leave[i].start())

    def theirs(d, crossing):
        far = inpl + d > PLANE - 1
        return jnp.logical_and(p + d <= last, far if crossing else jnp.logical_not(far))

    def take_bwd(d, crossing):
        nxt = jnp.minimum(d + 1, 7)
        have = theirs(d, crossing)
        onward = jnp.logical_and(jnp.logical_and(have, has_prev), d < 7)
        leave = bwd_step(d, (ob.at[d], lb.at[d], eb.at[d], sb.at[d]), p - 1, nxt,
                         lambda i: b_send.at[i, d])
        arrive = bwd_step(d, own_bwd, p, d, lambda i: b_send.at[i, 0])
        for i in range(4):
            pl.when(have)(lambda: arrive[i].wait_recv())
            pl.when(onward)(lambda: leave[i].start())

    half = 256
    mine = pl.ds(pl.multiple_of(c * half, half), half)
    quarter = [pl.ds(pl.multiple_of(c * half + q * 128, 128), 128) for q in range(2)]
    w_copies = []
    for i, (k, rows) in enumerate(
        ((1, mine), (NZ - 1, mine), (2, quarter[0]), (NZ - 2, quarter[1]))
    ):
        w_copies.append(
            copy_to(w_hbm.at[rows], wfull.at[f, rows], w_send.at[i], w_recv.at[i], *at_z(k)))
    start_all(w_copies)

    for one in loads:
        one.wait()

    def as_columns(row):
        return jnp.broadcast_to(row, (128, row.shape[1])).T

    lse_c[...] = as_columns(lse_ref[...])
    delta_c[...] = as_columns(delta_ref[...])
    docs_c[...] = as_columns(docs_ref[...].astype(F32)).astype(jnp.int32)
    dk_acc[...] = jnp.zeros_like(dk_acc)
    dv_acc[...] = jnp.zeros_like(dv_acc)

    take_fwd(1)
    pl.when(fwd_mid)(lambda: hand_on(via_fwd, mid_fwd))
    take_bwd(1, False)
    pl.when(bwd_mid)(lambda: hand_on(via_bwd, mid_bwd))

    f1, f2, f3 = lax.rem(f + 1, NF), lax.rem(f + 2, NF), lax.rem(f + 3, NF)
    wfull[f] = w_ref[...]

    def part(fs, w):
        cols = pl.ds(pl.multiple_of(fs * 512, 512), 512)
        return jnp.dot(h_ref[:, cols], w, preferred_element_type=F32)

    q_pre = part(f, w_ref[...])
    wc = [
        copy_to(wfull.at[fs, mine], wfull.at[fs, mine], wc_send.at[i], wc_recv.at[i], partner, f)
        for i, fs in enumerate((f3, f1, f2))
    ]
    w_copies[0].wait_recv()
    wc[0].start()
    w_copies[1].wait_recv()
    wc[1].start()
    w_copies[2].wait_recv()
    w_copies[3].wait_recv()
    wc[2].start()
    take_fwd(2)
    take_bwd(2, False)
    for i, fs in enumerate((f3, f1, f2)):
        wc[i].wait_recv()
        q_pre = q_pre + part(fs, wfull[fs])
    inv = lax.rsqrt(jnp.mean(q_pre * q_pre, axis=-1, keepdims=True) + 1e-06)
    normed = q_pre * inv
    q_own[...] = (normed * gain_ref[...]).astype(BF)
    normed_s[...] = normed
    inv_s[...] = jnp.broadcast_to(inv, inv_s.shape)

    def q_step(src, to, slot, send):
        return copy_to(src, qb.at[slot], send, q_recv.at[slot], to, f)

    first_q = q_step(q_own, p - 1, 1, q_send.at[0])
    home_q = q_step(q_own, bwd_to, bwd_far, qh_send)
    via_q = copy_to(q_own, hq, qh_send, hb_recv.at[4], bwd_mid_at, f)
    mid_q = q_step(hq, bwd_to, bwd_slot, hb_send.at[4])

    def dq_block(keys, values, docs_row, diagonal):
        for t in range(512 // TILE):
            rows = pl.ds(t * TILE, TILE)
            s = lax.dot_general(q_own[rows], keys[...], NT, preferred_element_type=F32) * scale
            allowed = wide(docs_c[rows]) == docs_row[...]
            if diagonal:
                i = lax.broadcasted_iota(jnp.int32, s.shape, 0) + t * TILE
                allowed = allowed & (i >= lax.broadcasted_iota(jnp.int32, s.shape, 1))
            prob = jnp.exp(jnp.where(allowed, s - wide(lse_c[rows]), -1e30))
            dp = lax.dot_general(do_ref[rows], values[...], NT, preferred_element_type=F32)
            ds = (prob * (dp - wide(delta_c[rows]))).astype(BF)
            term = jnp.dot(ds, keys[...], preferred_element_type=F32)
            if diagonal:
                dq_acc[rows] = term
            else:
                dq_acc[rows] += term

    dq_block(k_ref, v_ref, docs_ref, True)
    pl.when(has_prev)(lambda: first_q.start())
    pl.when(bwd_direct)(lambda: home_q.start())
    pl.when(bwd_via)(lambda: via_q.start())

    def take_q(d, crossing):
        have = theirs(d, crossing)

        @pl.when(have)
        def _():
            q_step(q_own, p, d, q_send.at[0]).wait_recv()

        @pl.when(jnp.logical_and(jnp.logical_and(have, has_prev), d < 7))
        def _():
            nxt = jnp.minimum(d + 1, 7)
            q_step(qb.at[d], p - 1, nxt, q_send.at[d]).start()

    def dq_far(d, carry):
        pl.when(p >= d)(lambda: dq_block(kb.at[d], vb.at[d], cb.at[d], False))
        return carry

    take_fwd(3)
    take_bwd(3, False)
    lax.fori_loop(1, 4, dq_far, 0)

    def chain(d, carry):
        take_fwd(d)
        take_bwd(d, False)
        take_q(d - LAG, False)
        pl.when(jnp.logical_and(d == 5, bwd_mid))(lambda: hand_on([via_q], [mid_q]))
        return dq_far(d, carry)

    lax.fori_loop(4, 8, chain, 0)

    g = dq_acc[...] * scale * gain_ref[...]
    nrm = normed_s[...]
    grad_pre = inv_s[...] * (g - nrm * jnp.mean(g * nrm, axis=-1, keepdims=True))
    gp_ref[...] = grad_pre.astype(BF)
    gp_t = grad_pre.T.astype(BF)

    def product(side, fs):
        cols = pl.ds(pl.multiple_of(fs * 512 + side * 256, 256), 256)
        return jnp.dot(gp_t, h_ref[:, cols], preferred_element_type=F32)

    def dkv_block(q_ref, o_ref, lse_row, delta_row, docs_row, diagonal):
        for t in range(512 // TILE):
            rows = pl.ds(t * TILE, TILE)
            s = lax.dot_general(k_ref[rows], q_ref[...], NT, preferred_element_type=F32) * scale
            allowed = wide(docs_c[rows]) == docs_row[...]
            if diagonal:
                i = lax.broadcasted_iota(jnp.int32, s.shape, 0) + t * TILE
                allowed = allowed & (i <= lax.broadcasted_iota(jnp.int32, s.shape, 1))
            prob = jnp.exp(jnp.where(allowed, s - lse_row[...], -1e30))
            dp = lax.dot_general(v_ref[rows], o_ref[...], NT, preferred_element_type=F32)
            ds = (prob * (dp - delta_row[...])).astype(BF)
            dv_acc[rows] += jnp.dot(prob.astype(BF), o_ref[...], preferred_element_type=F32)
            dk_acc[rows] += jnp.dot(ds, q_ref[...], preferred_element_type=F32)

    def filler(lo, hi, crossing):
        def one(d, carry):
            pl.when(theirs(d, crossing))(
                lambda: dkv_block(qb.at[d], ob.at[d], lb.at[d], eb.at[d], sb.at[d], False))
            return carry

        lax.fori_loop(lo, hi, one, 0)

    def cross(lo, hi):
        def one(d, carry):
            take_bwd(d, True)
            take_q(d, True)
            return carry

        lax.fori_loop(lo, hi, one, 0)

    for fs in range(NF):
        csend[:, fs * 256:(fs + 1) * 256] = product(1 - c, fs).astype(BF)
    to_core = copy_to(csend, crecv, c_sem.at[0], c_sem.at[1], partner, f)
    to_core.start()
    take_q(5, False)
    for fs in range(NF):
        own_half[:, fs * 256:(fs + 1) * 256] = product(c, fs)
    to_core.wait_recv()
    acc = own_half[...] + crecv[...].astype(F32)
    acc_s[...] = acc
    for xx in range(NX):
        xs[xx] = acc[32 * xx:32 * xx + 32].astype(BF)
    x_copies = [
        copy_to(xs.at[lax.rem(x + k, NX)], xr.at[k - 1], x_send.at[k - 1], x_recv.at[k - 1],
                at_x(k), f)
        for k in range(1, NX)
    ]
    start_all(x_copies)
    take_q(6, False)
    dkv_block(q_own, do_ref, lse_ref, delta_ref, docs_ref, True)
    a2 = acc_s[pl.ds(pl.multiple_of(32 * x, 32), 32), :]
    for k in range(NX - 1):
        x_copies[k].wait_recv()
        a2 = a2 + xr[k].astype(F32)
    for yy in range(NY):
        for fs in range(NF):
            col = fs * 256 + 128 * (yy % 2)
            y_own[yy, 8 * fs:8 * fs + 8] = a2[8 * (yy // 2):8 * (yy // 2) + 8, col:col + 128]
        ys[yy] = y_own[yy].astype(BF)
    y_copies = [
        copy_to(ys.at[lax.rem(y + k, NY)], yr.at[k - 1], y_send.at[k - 1], y_recv.at[k - 1],
                at_y(k), f)
        for k in range(1, NY)
    ]
    start_all(y_copies)
    take_q(7, False)
    filler(1, 4, False)
    a3 = y_own[y]
    for k in range(NY - 1):
        y_copies[k].wait_recv()
        a3 = a3 + yr[k].astype(F32)
    zs[...] = a3
    z_copies = []
    for k in range(1, NZ):
        blk, fz = at_z(k)
        z_copies.append(
            copy_to(zs.at[pl.ds(pl.multiple_of(8 * fz, 8), 8)], zr.at[k - 1], z_send.at[k - 1],
                    z_recv.at[k - 1], blk, fz))
    start_all(z_copies)
    cross(1, 5)
    filler(4, 8, False)
    filler(1, 5, True)
    done = zs[pl.ds(pl.multiple_of(8 * f, 8), 8), :]
    for k in range(NZ - 1):
        z_copies[k].wait_recv()
        done = done + zr[k]
    g1[y // 2, lax.rem(y, 2)] = done
    gy = [
        copy_to(g1.at[y // 2, lax.rem(y, 2)], g1.at[y // 2, lax.rem(y, 2)], gy_send.at[k - 1], gy_recv.at[k - 1], at_y(k), f)
        for k in range(1, NY)
    ]
    start_all(gy)
    cross(5, 8)
    filler(5, 8, True)
    for fs in range(NF):
        gh_ref[:, fs * 512:(fs + 1) * 512] = lax.dot_general(
            gp_ref[...], wfull[fs], NT, preferred_element_type=F32).astype(BF)
    dk_ref[...] = (dk_acc[...] * scale).astype(BF)
    dv_ref[...] = dv_acc[...].astype(BF)
    for one in gy:
        one.wait_recv()
    gx = [
        copy_to(g1, g2.at[x], gx_send.at[k - 1], gx_recv.at[k - 1], at_x(k), f)
        for k in range(1, NX)
    ]
    start_all(gx)
    g2[x] = g1[...]
    for one in gx:
        one.wait_recv()
    gc = copy_to(g2, g3.at[c], gc_sem.at[0], gc_sem.at[1], partner, f)
    gc.start()
    g3[c] = g2[...]

    pl.when(has_next)(lambda: finish_sends(first_fwd))
    pl.when(fwd_direct)(lambda: finish_sends(home_fwd))
    pl.when(fwd_via)(lambda: finish_sends(via_fwd))
    pl.when(fwd_mid)(lambda: finish_sends(mid_fwd))
    pl.when(has_prev)(lambda: finish_sends(first_bwd))
    pl.when(bwd_direct)(lambda: finish_sends(home_bwd + [home_q]))
    pl.when(bwd_via)(lambda: finish_sends(via_bwd + [via_q]))
    pl.when(bwd_mid)(lambda: finish_sends(mid_bwd + [mid_q]))
    pl.when(has_prev)(lambda: first_q.wait_send())
    finish_sends(w_copies)
    finish_sends(wc)

    def drained(d, carry):
        @pl.when(jnp.logical_and(p >= d, has_next))
        def _():
            finish_sends(fwd_step(d, (kb.at[d], vb.at[d], cb.at[d]), p + 1, d + 1,
                                  lambda i: f_send.at[i, d]))

        @pl.when(jnp.logical_and(p + d <= last, has_prev))
        def _():
            finish_sends(bwd_step(d, (ob.at[d], lb.at[d], eb.at[d], sb.at[d]), p - 1, d + 1,
                                  lambda i: b_send.at[i, d]))
            q_step(qb.at[d], p - 1, d + 1, q_send.at[d]).wait_send()

        return carry

    lax.fori_loop(1, 7, drained, 0)
    for group in ([to_core], x_copies, y_copies, z_copies, gy, gx, [gc]):
        finish_sends(group)
    gc.wait_recv()


def final_kernel(gh_ref, dk_ref, dv_ref, g_ref, gh_out, dk_out, dv_out, wq_out, wq, sem):
    puts = [
        pltpu.make_async_copy(src, dst, sem.at[i])
        for i, (src, dst) in enumerate(
            ((gh_ref, gh_out), (dk_ref, dk_out), (dv_ref, dv_out), (wq, wq_out)))
    ]
    for one in puts[:3]:
        one.start()
    for i in range(4):
        block = g_ref[i // 2, :, :, i % 2].reshape(128, 128)
        wq[i * 128:(i + 1) * 128, :] = block.T
    puts[3].start()
    for one in puts:
        one.wait()


def local(
    hidden_in, w_query, query_gain, key_rows, value_rows, grad_out, logsumexp, row_delta, doc_ids
):
    vmem = pl.BlockSpec(memory_space=pltpu.VMEM)
    hbm = pl.BlockSpec(memory_space=pltpu.HBM)
    sds = jax.ShapeDtypeStruct
    dma = pltpu.SemaphoreType.DMA
    v = pltpu.VMEM
    tok = (512, 128)
    gh, dk, dv, g3 = pl.pallas_call(
        main_kernel,
        out_shape=[sds((512, 2048), BF), sds(tok, BF), sds(tok, BF),
                   sds((2, NX, NY // 2, 2, 8, 128), F32)],
        in_specs=[hbm] * 9,
        out_specs=[vmem] * 4,
        scratch_shapes=[
            v((512, 2048), BF), v(tok, BF), v((1, 128), F32), v(tok, BF), v(tok, BF), v(tok, BF),
            v((1, 512), F32), v((1, 512), F32), v((1, 512), jnp.int32),
            v((NF, 512, 128), BF), v(tok, BF), v((8, *tok), BF), v((8, *tok), BF), v((8, 1, 512), jnp.int32),
            v((8, *tok), BF), v((8, 1, 512), F32), v((8, 1, 512), F32),
            v((8, 1, 512), jnp.int32), v((8, *tok), BF),
            v(tok, BF), v(tok, F32), v(tok, F32), v(tok, F32), v(tok, F32),
            v(tok, jnp.int32), v(tok, F32), v(tok, F32), v(tok, F32),
            v((128, 1024), F32), v((128, 1024), BF), v((128, 1024), BF), v((128, 1024), F32),
            v((NX, 32, 1024), BF), v((NX - 1, 32, 1024), BF), v((NY, 32, 128), F32),
            v((NY, 32, 128), BF), v((NY - 1, 32, 128), BF),
            v((32, 128), F32), v((NZ - 1, 8, 128), F32),
            v((NY // 2, 2, 8, 128), F32), v((NX, NY // 2, 2, 8, 128), F32),
            v(tok, BF), v(tok, BF), v((1, 512), jnp.int32), v(tok, BF), v((1, 512), F32),
            v((1, 512), F32), v((1, 512), jnp.int32), v(tok, BF),
            dma((9,)), dma((3, 8)), dma((3, 8)), dma((4, 8)), dma((4, 8)), dma((3,)), dma((4,)),
            dma((8,)), dma((8,)), dma, dma((3,)), dma((3,)), dma((5,)), dma((5,)),
            dma((4,)), dma((4,)), dma((3,)), dma((3,)), dma((2,)),
            dma((NX - 1,)), dma((NX - 1,)), dma((NY - 1,)), dma((NY - 1,)),
            dma((NZ - 1,)), dma((NZ - 1,)), dma((NY - 1,)), dma((NY - 1,)),
            dma((NX - 1,)), dma((NX - 1,)), dma((2,)),
        ],
        compiler_params=pltpu.CompilerParams(
            collective_id=0, has_side_effects=True, vmem_limit_bytes=40 << 20),
        name="main",
    )(*(pltpu.with_memory_space_constraint(a, pltpu.HBM) for a in (
        hidden_in[0], w_query, query_gain[None], key_rows[0], value_rows[0], grad_out[0],
        logsumexp, row_delta, doc_ids)))

    gh, dk, dv, wq = pl.pallas_call(
        final_kernel,
        out_shape=[sds((512, 2048), BF), sds(tok, BF), sds(tok, BF), sds(tok, F32)],
        in_specs=[vmem] * 4,
        out_specs=[hbm] * 4,
        scratch_shapes=[v(tok, F32), dma((4,))],
        compiler_params=pltpu.CompilerParams(vmem_limit_bytes=4 << 20),
        name="finish",
    )(gh, dk, dv, g3)
    return gh[None], dk[None], dv[None], wq


def solution(mesh):
    return jax.shard_map(
        local,
        mesh=mesh,
        in_specs=(
            P("fsdp", "blk", None),
            P("fsdp", None),
            P(),
            P("fsdp", "blk", None),
            P("fsdp", "blk", None),
            P("fsdp", "blk", None),
            P("fsdp", "blk"),
            P("fsdp", "blk"),
            P("fsdp", "blk"),
        ),
        out_specs=(
            P("fsdp", "blk", None),
            P("fsdp", "blk", None),
            P("fsdp", "blk", None),
            P("fsdp", None),
        ),
        check_vma=False,
    )
```

```python
import jax
import jax.numpy as jnp
from jax import lax
from jax.experimental import pallas as pl
from jax.experimental.pallas import tpu as pltpu
from jax.sharding import PartitionSpec as P

ROUNDS = 8
NX, NY, NZ, NF = 4, 8, 12, 4
PLANE = NX * NY * 2
GIVER = {1: 63, 2: 46, 3: 61, 4: 28, 5: 11, 6: 42, 7: 57}
HOME = {d: PLANE - d for d in GIVER}
DIRECT = [d for d in GIVER if GIVER[d] == HOME[d]]
VIA = [d for d in GIVER if GIVER[d] != HOME[d]]
MESH = pl.DeviceIdType.MESH
BF = jnp.bfloat16
F32 = jnp.float32
NT = (((1,), (1,)), ((), ()))
TILE = 512


def copy_to(src, dst, send, recv, blk, fsdp):
    return pltpu.make_async_remote_copy(
        src_ref=src, dst_ref=dst, send_sem=send, recv_sem=recv,
        device_id={"blk": blk, "fsdp": fsdp}, device_id_type=MESH)


def wide(column):
    return jnp.concatenate([column] * 4, axis=1)


def main_kernel(
    h_hbm, w_hbm, gain_hbm, k_hbm, v_hbm, do_hbm, lse_hbm, delta_hbm, docs_hbm,
    gh_ref, dk_ref, dv_ref, g3,
    h_ref, w_ref, gain_ref, k_ref, v_ref, do_ref, lse_ref, delta_ref, docs_ref,
    wfull, gp_ref, kb, vb, cb, ob, lb, eb, sb, qb,
    q_own, inv_s, normed_s, lse_c, delta_c, docs_c, dq_acc, dk_acc, dv_acc,
    own_half, csend, crecv, acc_s, xs, xr, y_own, ys, yr, zs, zr, g1, g2,
    hk, hv, hc, ho, hl, he, hs, hq,
    l_sem, f_send, f_recv, b_send, b_recv, fh_send, bh_send, q_send, q_recv, qh_send,
    hf_send, hf_recv, hb_send, hb_recv,
    w_send, w_recv, wc_send, wc_recv, c_sem, x_send, x_recv, y_send, y_recv, z_send, z_recv,
    gy_send, gy_recv, gx_send, gx_recv, gc_sem,
):
    p = lax.axis_index("blk")
    f = lax.axis_index("fsdp")
    last = lax.axis_size("blk") - 1
    c = lax.rem(p, 2)
    y = lax.rem(p // 2, NY)
    x = lax.rem(p // (2 * NY), NX)
    zh = p // PLANE
    z = zh * NF + f
    inpl = lax.rem(p, PLANE)
    scale = 128 ** -0.5

    def at_y(k):
        return p - 2 * y + 2 * lax.rem(y + k, NY)

    def at_x(k):
        return p - 2 * NY * x + 2 * NY * lax.rem(x + k, NX)

    def at_z(k):
        zz = lax.rem(z + k, NZ)
        return inpl + PLANE * (zz // NF), lax.rem(zz, NF)

    partner = p + 1 - 2 * c
    loads = [
        pltpu.make_async_copy(src, dst, l_sem.at[i])
        for i, (src, dst) in enumerate((
            (w_hbm, w_ref), (h_hbm, h_ref), (k_hbm, k_ref), (v_hbm, v_ref), (do_hbm, do_ref),
            (lse_hbm, lse_ref), (delta_hbm, delta_ref), (docs_hbm, docs_ref),
            (gain_hbm, gain_ref)))
    ]
    for one in loads:
        one.start()

    has_next = jnp.logical_and(p < last, inpl != PLANE - 1)
    has_prev = inpl != 0
    up, down = zh < NZ // NF - 1, zh > 0
    mirror = PLANE - 1 - inpl

    def among(values, at):
        hit = at == values[0]
        for one in values[1:]:
            hit = jnp.logical_or(hit, at == one)
        return hit

    def lookup(pairs, at):
        out = jnp.int32(0)
        for key, value in pairs:
            out = out + jnp.where(at == key, value, 0)
        return out

    def roles(on, at):
        direct = jnp.logical_and(on, among([HOME[d] for d in DIRECT], at))
        via = jnp.logical_and(on, among([HOME[d] for d in VIA], at))
        middle = jnp.logical_and(on, among([GIVER[d] for d in VIA], at))
        to_middle = lookup([(HOME[d], GIVER[d] - HOME[d]) for d in VIA], at)
        to_home = lookup([(GIVER[d], HOME[d] - GIVER[d]) for d in VIA], at)
        slot = lookup([(GIVER[d], d) for d in VIA], at)
        return direct, via, middle, to_middle, to_home, slot

    fwd_direct, fwd_via, fwd_mid, off, back, fwd_slot = roles(up, inpl)
    fwd_mid_at, fwd_home_at = p + off, p + back
    bwd_direct, bwd_via, bwd_mid, off, back, bwd_slot = roles(down, mirror)
    bwd_mid_at, bwd_home_at = p - off, p - back
    fwd_gate = jnp.logical_and(inpl == 0, p > 0)
    bwd_gate = jnp.logical_and(inpl == PLANE - 1, p < last)
    fwd_to = (zh + 1) * PLANE
    bwd_to = zh * PLANE - 1

    barrier = pltpu.get_barrier_semaphore()

    def greet(blk, fsdp):
        pl.semaphore_signal(
            barrier, inc=1, device_id={"blk": blk, "fsdp": fsdp}, device_id_type=MESH)

    greet(partner, f)
    for k in range(1, NY):
        greet(at_y(k), f)
    for k in range(1, NX):
        greet(at_x(k), f)
    for k in range(1, NZ):
        greet(*at_z(k))
    pl.when(has_next)(lambda: greet(p + 1, f))
    pl.when(has_prev)(lambda: greet(p - 1, f))
    pl.when(jnp.logical_or(fwd_direct, fwd_mid))(lambda: greet(fwd_to, f))
    pl.when(jnp.logical_or(bwd_direct, bwd_mid))(lambda: greet(bwd_to, f))
    pl.when(fwd_via)(lambda: greet(fwd_mid_at, f))
    pl.when(fwd_mid)(lambda: greet(fwd_home_at, f))
    pl.when(bwd_via)(lambda: greet(bwd_mid_at, f))
    pl.when(bwd_mid)(lambda: greet(bwd_home_at, f))

    @pl.when(fwd_gate)
    def _():
        for d in GIVER:
            greet(p - PLANE + GIVER[d], f)

    @pl.when(bwd_gate)
    def _():
        for d in GIVER:
            greet(p + PLANE - GIVER[d], f)

    peers = 1 + (NY - 1) + (NX - 1) + (NZ - 1)
    for flag, n in (
        (has_next, 1), (has_prev, 1), (fwd_direct, 1), (bwd_direct, 1), (fwd_mid, 2),
        (bwd_mid, 2), (fwd_via, 1), (bwd_via, 1), (fwd_gate, 7), (bwd_gate, 7),
    ):
        peers = peers + jnp.where(flag, n, 0)
    pl.semaphore_wait(barrier, peers)

    fwd_far = PLANE - inpl
    bwd_far = inpl + 1

    def fwd_step(d, srcs, to, slot, send):
        return [
            copy_to(src, buf.at[slot], send(i), f_recv.at[i, slot], to, f)
            for i, (src, buf) in enumerate(zip(srcs, (kb, vb, cb)))
        ]

    def bwd_step(d, srcs, to, slot, send):
        return [
            copy_to(src, buf.at[slot], send(i), b_recv.at[i, slot], to, f)
            for i, (src, buf) in enumerate(zip(srcs, (ob, lb, eb, sb)))
        ]

    own_fwd = (k_hbm, v_hbm, docs_hbm)
    own_bwd = (do_hbm, lse_hbm, delta_hbm, docs_hbm)
    first_fwd = fwd_step(0, own_fwd, p + 1, 1, lambda i: f_send.at[i, 0])
    home_fwd = fwd_step(0, own_fwd, fwd_to, fwd_far, lambda i: fh_send.at[i])
    via_fwd = [
        copy_to(src, buf, fh_send.at[i], hf_recv.at[i], fwd_mid_at, f)
        for i, (src, buf) in enumerate(zip(own_fwd, (hk, hv, hc)))
    ]
    mid_fwd = fwd_step(0, (hk, hv, hc), fwd_to, fwd_slot, lambda i: hf_send.at[i])
    first_bwd = bwd_step(0, own_bwd, p - 1, 1, lambda i: b_send.at[i, 0])
    home_bwd = bwd_step(0, own_bwd, bwd_to, bwd_far, lambda i: bh_send.at[i])
    via_bwd = [
        copy_to(src, buf, bh_send.at[i], hb_recv.at[i], bwd_mid_at, f)
        for i, (src, buf) in enumerate(zip(own_bwd, (ho, hl, he, hs)))
    ]
    mid_bwd = bwd_step(0, (ho, hl, he, hs), bwd_to, bwd_slot, lambda i: hb_send.at[i])

    def start_all(copies):
        for one in copies:
            one.start()

    def finish_sends(copies):
        for one in copies:
            one.wait_send()

    def hand_on(arriving, leaving):
        for i in range(len(leaving)):
            arriving[i].wait_recv()
            leaving[i].start()

    pl.when(fwd_direct)(lambda: start_all(home_fwd))
    pl.when(fwd_via)(lambda: start_all(via_fwd))
    pl.when(has_next)(lambda: start_all(first_fwd))
    pl.when(bwd_direct)(lambda: start_all(home_bwd))
    pl.when(bwd_via)(lambda: start_all(via_bwd))
    pl.when(has_prev)(lambda: start_all(first_bwd))

    def take_fwd(d):
        nxt = jnp.minimum(d + 1, 7)
        have = p >= d
        onward = jnp.logical_and(jnp.logical_and(have, has_next), d < 7)
        leave = fwd_step(d, (kb.at[d], vb.at[d], cb.at[d]), p + 1, nxt, lambda i: f_send.at[i, d])
        arrive = fwd_step(d, own_fwd, p, d, lambda i: f_send.at[i, 0])
        for i in range(3):
            pl.when(have)(lambda: arrive[i].wait_recv())
            pl.when(onward)(lambda: leave[i].start())

    def theirs(d, crossing):
        far = inpl + d > PLANE - 1
        return jnp.logical_and(p + d <= last, far if crossing else jnp.logical_not(far))

    def take_bwd(d, crossing):
        nxt = jnp.minimum(d + 1, 7)
        have = theirs(d, crossing)
        onward = jnp.logical_and(jnp.logical_and(have, has_prev), d < 7)
        leave = bwd_step(d, (ob.at[d], lb.at[d], eb.at[d], sb.at[d]), p - 1, nxt,
                         lambda i: b_send.at[i, d])
        arrive = bwd_step(d, own_bwd, p, d, lambda i: b_send.at[i, 0])
        for i in range(4):
            pl.when(have)(lambda: arrive[i].wait_recv())
            pl.when(onward)(lambda: leave[i].start())

    half = 256
    mine = pl.ds(pl.multiple_of(c * half, half), half)
    quarter = [pl.ds(pl.multiple_of(c * half + q * 128, 128), 128) for q in range(2)]
    w_copies = []
    for i, (k, rows) in enumerate(
        ((1, mine), (NZ - 1, mine), (2, quarter[0]), (NZ - 2, quarter[1]))
    ):
        w_copies.append(
            copy_to(w_hbm.at[rows], wfull.at[f, rows], w_send.at[i], w_recv.at[i], *at_z(k)))
    start_all(w_copies)

    for one in loads:
        one.wait()

    def as_columns(row):
        return jnp.broadcast_to(row, (128, row.shape[1])).T

    lse_c[...] = as_columns(lse_ref[...])
    delta_c[...] = as_columns(delta_ref[...])
    docs_c[...] = as_columns(docs_ref[...].astype(F32)).astype(jnp.int32)
    dk_acc[...] = jnp.zeros_like(dk_acc)
    dv_acc[...] = jnp.zeros_like(dv_acc)

    take_fwd(1)
    pl.when(fwd_mid)(lambda: hand_on(via_fwd, mid_fwd))
    pl.when(bwd_mid)(lambda: hand_on(via_bwd, mid_bwd))

    f1, f2, f3 = lax.rem(f + 1, NF), lax.rem(f + 2, NF), lax.rem(f + 3, NF)
    wfull[f] = w_ref[...]

    def part(fs, w):
        cols = pl.ds(pl.multiple_of(fs * 512, 512), 512)
        return jnp.dot(h_ref[:, cols], w, preferred_element_type=F32)

    q_pre = part(f, w_ref[...])
    wc = [
        copy_to(wfull.at[fs, mine], wfull.at[fs, mine], wc_send.at[i], wc_recv.at[i], partner, f)
        for i, fs in enumerate((f3, f1, f2))
    ]
    w_copies[0].wait_recv()
    wc[0].start()
    w_copies[1].wait_recv()
    wc[1].start()
    w_copies[2].wait_recv()
    w_copies[3].wait_recv()
    wc[2].start()
    take_fwd(2)
    for i, fs in enumerate((f3, f1, f2)):
        wc[i].wait_recv()
        q_pre = q_pre + part(fs, wfull[fs])
    inv = lax.rsqrt(jnp.mean(q_pre * q_pre, axis=-1, keepdims=True) + 1e-06)
    normed = q_pre * inv
    q_own[...] = (normed * gain_ref[...]).astype(BF)
    normed_s[...] = normed
    inv_s[...] = jnp.broadcast_to(inv, inv_s.shape)

    def q_step(src, to, slot, send):
        return copy_to(src, qb.at[slot], send, q_recv.at[slot], to, f)

    first_q = q_step(q_own, p - 1, 1, q_send.at[0])
    home_q = q_step(q_own, bwd_to, bwd_far, qh_send)
    via_q = copy_to(q_own, hq, qh_send, hb_recv.at[4], bwd_mid_at, f)
    mid_q = q_step(hq, bwd_to, bwd_slot, hb_send.at[4])

    def dq_block(keys, values, docs_row, diagonal):
        for t in range(512 // TILE):
            rows = pl.ds(t * TILE, TILE)
            s = lax.dot_general(q_own[rows], keys[...], NT, preferred_element_type=F32) * scale
            allowed = wide(docs_c[rows]) == docs_row[...]
            if diagonal:
                i = lax.broadcasted_iota(jnp.int32, s.shape, 0) + t * TILE
                allowed = allowed & (i >= lax.broadcasted_iota(jnp.int32, s.shape, 1))
            prob = jnp.exp(jnp.where(allowed, s - wide(lse_c[rows]), -1e30))
            dp = lax.dot_general(do_ref[rows], values[...], NT, preferred_element_type=F32)
            ds = (prob * (dp - wide(delta_c[rows]))).astype(BF)
            term = jnp.dot(ds, keys[...], preferred_element_type=F32)
            if diagonal:
                dq_acc[rows] = term
            else:
                dq_acc[rows] += term

    dq_block(k_ref, v_ref, docs_ref, True)
    pl.when(has_prev)(lambda: first_q.start())
    pl.when(bwd_direct)(lambda: home_q.start())
    pl.when(bwd_via)(lambda: via_q.start())

    def take_q(d, crossing):
        have = theirs(d, crossing)

        @pl.when(have)
        def _():
            q_step(q_own, p, d, q_send.at[0]).wait_recv()

        @pl.when(jnp.logical_and(jnp.logical_and(have, has_prev), d < 7))
        def _():
            nxt = jnp.minimum(d + 1, 7)
            q_step(qb.at[d], p - 1, nxt, q_send.at[d]).start()

    def take_rows(d):
        take_bwd(d, False)
        take_q(d, False)

    def dq_far(d, carry):
        pl.when(p >= d)(lambda: dq_block(kb.at[d], vb.at[d], cb.at[d], False))
        return carry

    take_fwd(3)
    lax.fori_loop(1, 4, dq_far, 0)

    def chain(d, carry):
        take_fwd(d)
        pl.when(lax.rem(d, 2) == 0)(lambda: take_rows(d // 2 - 1))
        pl.when(jnp.logical_and(d == 5, bwd_mid))(lambda: hand_on([via_q], [mid_q]))
        return dq_far(d, carry)

    lax.fori_loop(4, 8, chain, 0)

    g = dq_acc[...] * scale * gain_ref[...]
    nrm = normed_s[...]
    grad_pre = inv_s[...] * (g - nrm * jnp.mean(g * nrm, axis=-1, keepdims=True))
    gp_ref[...] = grad_pre.astype(BF)
    gp_t = grad_pre.T.astype(BF)

    def product(side, fs):
        cols = pl.ds(pl.multiple_of(fs * 512 + side * 256, 256), 256)
        return jnp.dot(gp_t, h_ref[:, cols], preferred_element_type=F32)

    def dkv_block(q_ref, o_ref, lse_row, delta_row, docs_row, diagonal):
        for t in range(512 // TILE):
            rows = pl.ds(t * TILE, TILE)
            s = lax.dot_general(k_ref[rows], q_ref[...], NT, preferred_element_type=F32) * scale
            allowed = wide(docs_c[rows]) == docs_row[...]
            if diagonal:
                i = lax.broadcasted_iota(jnp.int32, s.shape, 0) + t * TILE
                allowed = allowed & (i <= lax.broadcasted_iota(jnp.int32, s.shape, 1))
            prob = jnp.exp(jnp.where(allowed, s - lse_row[...], -1e30))
            dp = lax.dot_general(v_ref[rows], o_ref[...], NT, preferred_element_type=F32)
            ds = (prob * (dp - delta_row[...])).astype(BF)
            dv_acc[rows] += jnp.dot(prob.astype(BF), o_ref[...], preferred_element_type=F32)
            dk_acc[rows] += jnp.dot(ds, q_ref[...], preferred_element_type=F32)

    def filler(lo, hi, crossing):
        def one(d, carry):
            pl.when(theirs(d, crossing))(
                lambda: dkv_block(qb.at[d], ob.at[d], lb.at[d], eb.at[d], sb.at[d], False))
            return carry

        lax.fori_loop(lo, hi, one, 0)

    before = PLANE - 1 - inpl
    turn = (before + 1) // 2

    def cross(k):
        def take(d, carry):
            @pl.when(turn == k)
            def _():
                take_bwd(d, True)
                take_q(d, True)

            return carry

        def use(d, carry):
            pl.when(jnp.logical_and(turn == k, theirs(d, True)))(
                lambda: dkv_block(qb.at[d], ob.at[d], lb.at[d], eb.at[d], sb.at[d], False))
            return carry

        lax.fori_loop(1, 8, take, 0)
        lax.fori_loop(1, 8, use, 0)

    for fs in range(NF):
        csend[:, fs * 256:(fs + 1) * 256] = product(1 - c, fs).astype(BF)
    to_core = copy_to(csend, crecv, c_sem.at[0], c_sem.at[1], partner, f)
    to_core.start()
    take_rows(3)
    for fs in range(NF):
        own_half[:, fs * 256:(fs + 1) * 256] = product(c, fs)
    to_core.wait_recv()
    acc = own_half[...] + crecv[...].astype(F32)
    acc_s[...] = acc
    for xx in range(NX):
        xs[xx] = acc[32 * xx:32 * xx + 32].astype(BF)
    x_copies = [
        copy_to(xs.at[lax.rem(x + k, NX)], xr.at[k - 1], x_send.at[k - 1], x_recv.at[k - 1],
                at_x(k), f)
        for k in range(1, NX)
    ]
    start_all(x_copies)
    take_rows(4)
    dkv_block(q_own, do_ref, lse_ref, delta_ref, docs_ref, True)
    a2 = acc_s[pl.ds(pl.multiple_of(32 * x, 32), 32), :]
    for k in range(NX - 1):
        x_copies[k].wait_recv()
        a2 = a2 + xr[k].astype(F32)
    for yy in range(NY):
        for fs in range(NF):
            col = fs * 256 + 128 * (yy % 2)
            y_own[yy, 8 * fs:8 * fs + 8] = a2[8 * (yy // 2):8 * (yy // 2) + 8, col:col + 128]
        ys[yy] = y_own[yy].astype(BF)
    y_copies = [
        copy_to(ys.at[lax.rem(y + k, NY)], yr.at[k - 1], y_send.at[k - 1], y_recv.at[k - 1],
                at_y(k), f)
        for k in range(1, NY)
    ]
    start_all(y_copies)
    take_rows(5)
    filler(1, 4, False)
    cross(0)
    a3 = y_own[y]
    for k in range(NY - 1):
        y_copies[k].wait_recv()
        a3 = a3 + yr[k].astype(F32)
    zs[...] = a3
    z_copies = []
    for k in range(1, NZ):
        blk, fz = at_z(k)
        z_copies.append(
            copy_to(zs.at[pl.ds(pl.multiple_of(8 * fz, 8), 8)], zr.at[k - 1], z_send.at[k - 1],
                    z_recv.at[k - 1], blk, fz))
    start_all(z_copies)
    take_rows(6)
    filler(4, 6, False)
    take_rows(7)
    filler(6, 8, False)
    cross(1)
    done = zs[pl.ds(pl.multiple_of(8 * f, 8), 8), :]
    for k in range(NZ - 1):
        z_copies[k].wait_recv()
        done = done + zr[k]
    g1[y // 2, lax.rem(y, 2)] = done
    gy = [
        copy_to(g1.at[y // 2, lax.rem(y, 2)], g1.at[y // 2, lax.rem(y, 2)], gy_send.at[k - 1], gy_recv.at[k - 1], at_y(k), f)
        for k in range(1, NY)
    ]
    start_all(gy)
    cross(2)
    for fs in range(NF):
        gh_ref[:, fs * 512:(fs + 1) * 512] = lax.dot_general(
            gp_ref[...], wfull[fs], NT, preferred_element_type=F32).astype(BF)
    for one in gy:
        one.wait_recv()
    gx = [
        copy_to(g1, g2.at[x], gx_send.at[k - 1], gx_recv.at[k - 1], at_x(k), f)
        for k in range(1, NX)
    ]
    start_all(gx)
    g2[x] = g1[...]
    cross(3)
    dk_ref[...] = (dk_acc[...] * scale).astype(BF)
    dv_ref[...] = dv_acc[...].astype(BF)
    for one in gx:
        one.wait_recv()
    gc = copy_to(g2, g3.at[c], gc_sem.at[0], gc_sem.at[1], partner, f)
    gc.start()
    g3[c] = g2[...]

    pl.when(has_next)(lambda: finish_sends(first_fwd))
    pl.when(fwd_direct)(lambda: finish_sends(home_fwd))
    pl.when(fwd_via)(lambda: finish_sends(via_fwd))
    pl.when(fwd_mid)(lambda: finish_sends(mid_fwd))
    pl.when(has_prev)(lambda: finish_sends(first_bwd))
    pl.when(bwd_direct)(lambda: finish_sends(home_bwd + [home_q]))
    pl.when(bwd_via)(lambda: finish_sends(via_bwd + [via_q]))
    pl.when(bwd_mid)(lambda: finish_sends(mid_bwd + [mid_q]))
    pl.when(has_prev)(lambda: first_q.wait_send())
    finish_sends(w_copies)
    finish_sends(wc)

    def drained(d, carry):
        @pl.when(jnp.logical_and(p >= d, has_next))
        def _():
            finish_sends(fwd_step(d, (kb.at[d], vb.at[d], cb.at[d]), p + 1, d + 1,
                                  lambda i: f_send.at[i, d]))

        @pl.when(jnp.logical_and(p + d <= last, has_prev))
        def _():
            finish_sends(bwd_step(d, (ob.at[d], lb.at[d], eb.at[d], sb.at[d]), p - 1, d + 1,
                                  lambda i: b_send.at[i, d]))
            q_step(qb.at[d], p - 1, d + 1, q_send.at[d]).wait_send()

        return carry

    lax.fori_loop(1, 7, drained, 0)
    for group in ([to_core], x_copies, y_copies, z_copies, gy, gx, [gc]):
        finish_sends(group)
    gc.wait_recv()


def final_kernel(gh_ref, dk_ref, dv_ref, g_ref, gh_out, dk_out, dv_out, wq_out, wq, sem):
    puts = [
        pltpu.make_async_copy(src, dst, sem.at[i])
        for i, (src, dst) in enumerate(
            ((gh_ref, gh_out), (dk_ref, dk_out), (dv_ref, dv_out), (wq, wq_out)))
    ]
    for one in puts[:3]:
        one.start()
    for i in range(4):
        block = g_ref[i // 2, :, :, i % 2].reshape(128, 128)
        wq[i * 128:(i + 1) * 128, :] = block.T
    puts[3].start()
    for one in puts:
        one.wait()


def local(
    hidden_in, w_query, query_gain, key_rows, value_rows, grad_out, logsumexp, row_delta, doc_ids
):
    vmem = pl.BlockSpec(memory_space=pltpu.VMEM)
    hbm = pl.BlockSpec(memory_space=pltpu.HBM)
    sds = jax.ShapeDtypeStruct
    dma = pltpu.SemaphoreType.DMA
    v = pltpu.VMEM
    tok = (512, 128)
    gh, dk, dv, g3 = pl.pallas_call(
        main_kernel,
        out_shape=[sds((512, 2048), BF), sds(tok, BF), sds(tok, BF),
                   sds((2, NX, NY // 2, 2, 8, 128), F32)],
        in_specs=[hbm] * 9,
        out_specs=[vmem] * 4,
        scratch_shapes=[
            v((512, 2048), BF), v(tok, BF), v((1, 128), F32), v(tok, BF), v(tok, BF), v(tok, BF),
            v((1, 512), F32), v((1, 512), F32), v((1, 512), jnp.int32),
            v((NF, 512, 128), BF), v(tok, BF), v((8, *tok), BF), v((8, *tok), BF), v((8, 1, 512), jnp.int32),
            v((8, *tok), BF), v((8, 1, 512), F32), v((8, 1, 512), F32),
            v((8, 1, 512), jnp.int32), v((8, *tok), BF),
            v(tok, BF), v(tok, F32), v(tok, F32), v(tok, F32), v(tok, F32),
            v(tok, jnp.int32), v(tok, F32), v(tok, F32), v(tok, F32),
            v((128, 1024), F32), v((128, 1024), BF), v((128, 1024), BF), v((128, 1024), F32),
            v((NX, 32, 1024), BF), v((NX - 1, 32, 1024), BF), v((NY, 32, 128), F32),
            v((NY, 32, 128), BF), v((NY - 1, 32, 128), BF),
            v((32, 128), F32), v((NZ - 1, 8, 128), F32),
            v((NY // 2, 2, 8, 128), F32), v((NX, NY // 2, 2, 8, 128), F32),
            v(tok, BF), v(tok, BF), v((1, 512), jnp.int32), v(tok, BF), v((1, 512), F32),
            v((1, 512), F32), v((1, 512), jnp.int32), v(tok, BF),
            dma((9,)), dma((3, 8)), dma((3, 8)), dma((4, 8)), dma((4, 8)), dma((3,)), dma((4,)),
            dma((8,)), dma((8,)), dma, dma((3,)), dma((3,)), dma((5,)), dma((5,)),
            dma((4,)), dma((4,)), dma((3,)), dma((3,)), dma((2,)),
            dma((NX - 1,)), dma((NX - 1,)), dma((NY - 1,)), dma((NY - 1,)),
            dma((NZ - 1,)), dma((NZ - 1,)), dma((NY - 1,)), dma((NY - 1,)),
            dma((NX - 1,)), dma((NX - 1,)), dma((2,)),
        ],
        compiler_params=pltpu.CompilerParams(
            collective_id=0, has_side_effects=True, vmem_limit_bytes=40 << 20),
        name="main",
    )(*(pltpu.with_memory_space_constraint(a, pltpu.HBM) for a in (
        hidden_in[0], w_query, query_gain[None], key_rows[0], value_rows[0], grad_out[0],
        logsumexp, row_delta, doc_ids)))

    gh, dk, dv, wq = pl.pallas_call(
        final_kernel,
        out_shape=[sds((512, 2048), BF), sds(tok, BF), sds(tok, BF), sds(tok, F32)],
        in_specs=[vmem] * 4,
        out_specs=[hbm] * 4,
        scratch_shapes=[v(tok, F32), dma((4,))],
        compiler_params=pltpu.CompilerParams(vmem_limit_bytes=4 << 20),
        name="finish",
    )(gh, dk, dv, g3)
    return gh[None], dk[None], dv[None], wq


def solution(mesh):
    return jax.shard_map(
        local,
        mesh=mesh,
        in_specs=(
            P("fsdp", "blk", None),
            P("fsdp", None),
            P(),
            P("fsdp", "blk", None),
            P("fsdp", "blk", None),
            P("fsdp", "blk", None),
            P("fsdp", "blk"),
            P("fsdp", "blk"),
            P("fsdp", "blk"),
        ),
        out_specs=(
            P("fsdp", "blk", None),
            P("fsdp", "blk", None),
            P("fsdp", "blk", None),
            P("fsdp", None),
        ),
        check_vma=False,
    )
```
